32 devices in a mesh: dp: 8 (over z, y), space: 4 (over x, core).
Axes of the slice: x: 2, y: 2, z: 4, core: 2. Of those that a mesh axis runs over, the one named last changes fastest.
Arguments:
- volume: bfloat16 [8, 4, 32, 32, 32], P('dp', None, 'space'), may hold values from -6 to 6
- cotangent: bfloat16 [8, 64, 512], P('dp', None, 'space'), may hold values from -6 to 6
- conv_one: bfloat16 [32, 4, 3, 3, 3], replicated, may hold values from -0.625 to 0.625
- conv_two: bfloat16 [64, 32, 3, 3, 3], replicated, may hold values from -0.21875 to 0.21875
Outputs:
- out_two: bfloat16 [8, 64, 512], P('dp', None, 'space')
- grad_pre: bfloat16 [8, 32, 4096], P('dp', None, 'space')
- update_one: float32 [3456], replicated
- update_two: float32 [55296], replicated
The draws below stay inside these ranges and needn't reach their ends.
All inputs are finite; a program needn't handle non-finite values.
Results may differ from the reference program's by a relative error of at most 0.0057.
Values may be sent and summed in bfloat16 or wider, within the bound.
A program may use at most 64 MiB of HBM per device.

```python
import jax
import jax.numpy as jnp
from jax import lax

C0 = 4
C1 = 32
C2 = 64
S = 32
CROPS = 8
DEPTH = 32


def block_levels(own_key, shape, cuts, smallest, top_value):
    def one(position, blocks):
        steps = jax.random.uniform(jax.random.fold_in(jax.random.fold_in(own_key, 6), position), (blocks,), jnp.float32, smallest / len(cuts), top_value / len(cuts))
        return jnp.repeat(jnp.exp(steps), shape[position] // blocks).reshape((-1,) + (1,) * (len(shape) - position - 1))

    level = one(*cuts[0])
    for cut in cuts[1:]:
        level = level * one(*cut)
    return level


def noise(own_key, shape, width, limit, shards=(), kind=jnp.bfloat16):
    result = jax.random.normal(own_key, shape, jnp.float32) * width
    if len(shards) > 0:
        result = block_levels(own_key, shape, shards, -0.22, 0.18) * result
    return jnp.clip(result, min=-limit, max=limit).astype(kind)


def setup_inputs(seed: int = 0) -> dict:
    arg_keys = jax.random.split(jax.random.key(seed), 5)
    volume = noise(arg_keys[0], (CROPS, C0, DEPTH, S, S), 1.0, 6.0, ((0, 8), (2, 4)))
    cotangent = noise(arg_keys[1], (CROPS, C2, (DEPTH // 4) * (S // 4) * (S // 4)), 1.0, 6.0, ((0, 8), (2, 4)))
    conv_one = noise(arg_keys[2], (C1, C0, 3, 3, 3), (27 * C0) ** -0.5, 0.625)
    conv_two = noise(arg_keys[3], (C2, C1, 3, 3, 3), (27 * C1) ** -0.5, 0.21875)
    return {"volume": volume, "cotangent": cotangent, "conv_one": conv_one, "conv_two": conv_two}


damp_input = 0.1
damp_grad = 0.03

def tap_stack(padded, out_depth, out_rows, out_cols):
    pieces = []
    for depth_tap in range(3):
        for row_tap in range(3):
            for col_tap in range(3):
                pieces.append(padded[:, depth_tap:depth_tap + 2 * out_depth:2, row_tap:row_tap + 2 * out_rows:2, col_tap:col_tap + 2 * out_cols:2])
    stacked = jnp.stack(pieces, axis=1)
    return stacked.reshape(stacked.shape[0] * 27, -1)

def spread_taps(columns, channels, out_depth, out_rows, out_cols):
    pieces = columns.reshape(channels, 27, out_depth, out_rows, out_cols)
    canvas = jnp.zeros((channels, 2 * out_depth + 1, 2 * out_rows + 1, 2 * out_cols + 1), jnp.float32)
    for depth_tap in range(3):
        for row_tap in range(3):
            for col_tap in range(3):
                tap_number = depth_tap * 9 + row_tap * 3 + col_tap
                canvas = canvas.at[:, depth_tap:depth_tap + 2 * out_depth:2, row_tap:row_tap + 2 * out_rows:2, col_tap:col_tap + 2 * out_cols:2].add(pieces[:, tap_number])
    return canvas

def silu_slope(pre_act):
    sigmoid_val = jax.nn.sigmoid(pre_act)
    return sigmoid_val * (1.0 + pre_act * (1.0 - sigmoid_val))

def crop_pass(volume_crop, cot_crop, weight_one, weight_two):
    width_one = weight_one.shape[0]
    width_two = weight_two.shape[0]
    depth_len, row_count, col_count = (volume_crop.shape[1], volume_crop.shape[2], volume_crop.shape[3])
    padded = jnp.pad(volume_crop, ((0, 0), (1, 0), (1, 0), (1, 0)))
    first_cols = tap_stack(padded, depth_len // 2, row_count // 2, col_count // 2)
    pre_one = jnp.dot(weight_one.astype(jnp.float32), first_cols.astype(jnp.float32), preferred_element_type=jnp.float32)
    act_one = jax.nn.silu(pre_one).astype(jnp.bfloat16).reshape(width_one, depth_len // 2, row_count // 2, col_count // 2)
    padded_two = jnp.pad(act_one, ((0, 0), (1, 0), (1, 0), (1, 0)))
    second_cols = tap_stack(padded_two, depth_len // 4, row_count // 4, col_count // 4)
    out_two = jnp.dot(weight_two.astype(jnp.float32), second_cols.astype(jnp.float32), preferred_element_type=jnp.float32).astype(jnp.bfloat16)
    cot_flat = cot_crop.reshape(width_two, -1)
    back_cols = jnp.dot(weight_two.T.astype(jnp.float32), cot_flat.astype(jnp.float32), preferred_element_type=jnp.float32)
    canvas = spread_taps(back_cols, width_one, depth_len // 4, row_count // 4, col_count // 4)
    grad_act = canvas[:, 1:, 1:, 1:].reshape(width_one, -1)
    grad_pre = (grad_act * silu_slope(pre_one)).astype(jnp.bfloat16)
    stats = (jnp.dot(first_cols.astype(jnp.float32), first_cols.T.astype(jnp.float32), preferred_element_type=jnp.float32), jnp.dot(grad_pre.astype(jnp.float32), grad_pre.T.astype(jnp.float32), preferred_element_type=jnp.float32), jnp.dot(grad_pre.astype(jnp.float32), first_cols.T.astype(jnp.float32), preferred_element_type=jnp.float32), jnp.dot(second_cols.astype(jnp.float32), second_cols.T.astype(jnp.float32), preferred_element_type=jnp.float32), jnp.dot(cot_flat.astype(jnp.float32), cot_flat.T.astype(jnp.float32), preferred_element_type=jnp.float32), jnp.dot(cot_flat.astype(jnp.float32), second_cols.T.astype(jnp.float32), preferred_element_type=jnp.float32))
    return (out_two.reshape(cot_crop.shape), grad_pre, stats)

def precondition(gram_in, gram_out, grad_sum, total_rows):
    in_mat = gram_in / total_rows + damp_input * jnp.eye(gram_in.shape[0], dtype=jnp.float32)
    out_mat = gram_out / total_rows + damp_grad * jnp.eye(gram_out.shape[0], dtype=jnp.float32)
    mean_grad = grad_sum / total_rows
    half_solved = jnp.linalg.solve(in_mat, mean_grad.T).T
    return (jnp.linalg.solve(out_mat, half_solved), mean_grad)

def reference(volume, cotangent, conv_one, conv_two):
    weight_one = conv_one.reshape(conv_one.shape[0], -1)
    weight_two = conv_two.reshape(conv_two.shape[0], -1)
    crop_count = volume.shape[0]
    k_one = weight_one.shape[1]
    k_two = weight_two.shape[1]
    width_one = weight_one.shape[0]
    width_two = weight_two.shape[0]
    init = (jnp.zeros((k_one, k_one), jnp.float32), jnp.zeros((width_one, width_one), jnp.float32), jnp.zeros((width_one, k_one), jnp.float32), jnp.zeros((k_two, k_two), jnp.float32), jnp.zeros((width_two, width_two), jnp.float32), jnp.zeros((width_two, k_two), jnp.float32))

    def crop_step(carry, crop_pair):
        out_crop, grad_crop, stats = crop_pass(crop_pair[0], crop_pair[1], weight_one, weight_two)
        return (jax.tree.map(lambda left, right: left + right, carry, stats), (out_crop, grad_crop))
    sums, stacked = lax.scan(crop_step, init, (volume, cotangent))
    out_two, grad_pre = stacked
    total_one = crop_count * (volume.shape[2] // 2) * (volume.shape[3] // 2) * (volume.shape[4] // 2)
    total_two = crop_count * cotangent.shape[2]
    step_one, mean_one = precondition(sums[0], sums[1], sums[2], total_one)
    step_two, mean_two = precondition(sums[3], sums[4], sums[5], total_two)
    quad_form = jnp.sum(step_one * mean_one) + jnp.sum(step_two * mean_two)
    factor = jnp.sqrt((step_one.size + step_two.size) / quad_form)
    return (out_two, grad_pre, (factor * step_one).reshape(-1), (factor * step_two).reshape(-1))
```

```python
import jax
import jax.numpy as jnp
import numpy as np
from jax import lax
from jax.experimental import pallas as pl
from jax.experimental.pallas import tpu as pltpu
from jax.sharding import PartitionSpec as P

damp_input = 0.1
damp_grad = 0.03
TOLERANCE = 1e-6
MAX_STEPS = 5000
CELLS = 128
PLANE = 64
BLOCKS_ONE = [(sd, sh, sw) for sd in (0, 1) for sh in (0, 1) for sw in (0, 1)]
TAPS = [(a, b, e) for a in range(3) for b in range(3) for e in range(3)]
PHASES = [(d, h, w) for d in (0, 1) for h in (0, 1) for w in (0, 1)]
SUBROWS = 896


def block_rows():
    table, row = {}, 0
    for sd, sh, sw in BLOCKS_ONE:
        for md in (3,) if sd else range(4):
            for mh in (3,) if sh else range(4):
                for mw in range(4):
                    for c in range(4):
                        table[(sd, sh, sw, md, mh, mw, c)] = row
                        row += 1
    return table


def selection():
    table = block_rows()
    sel = np.zeros((8 * 128, SUBROWS), np.float32)
    for ph, (dp, hp, wp) in enumerate(PHASES):
        for c in range(4):
            for t, (a, b, e) in enumerate(TAPS):
                offs = [2 * dp + a - 1, 2 * hp + b - 1, 2 * wp + e - 1]
                sh = [int(o < 0) for o in offs]
                md = [o % 4 for o in offs]
                sel[ph * 128 + c * 27 + t, table[(*sh, *md, c)]] = 1.0
    return sel


def dot(left, right):
    return jnp.dot(left, right, preferred_element_type=jnp.float32)


def dot_t(left, right):
    return lax.dot_general(left, right, (((1,), (1,)), ((), ())), preferred_element_type=jnp.float32)


def patches_two(act, p_idx, q_idx, tap):
    a, b, e = tap
    ph = 4 * (a != 1) + 2 * (b != 1) + (e != 1)
    shift = 64 * (a == 0) + 8 * (b == 0) + (e == 0)
    rows = act[ph * 32 : ph * 32 + 32]
    if shift:
        rows = pltpu.roll(rows, shift, 1)
    rows = rows[:, CELLS:]
    if b == 0:
        rows = jnp.where(p_idx == 0, 0.0, rows)
    if e == 0:
        rows = jnp.where(q_idx == 0, 0.0, rows)
    return rows.astype(jnp.bfloat16)


def local_kernel(
    v_ref, c_ref, sel_ref, w1_ref, w2_ref, w2t_ref,
    out_ref, e1_ref, in_two_ref, grad_two_ref, small_ref,
    x_ref, p1_ref, p2_ref,
):
    lane = lax.broadcasted_iota(jnp.int32, (256, 256), 1)
    p_all = (lane // 8) % 8
    q_all = lane % 8
    vol = v_ref[...].astype(jnp.float32)
    row = 0
    for sd, sh, sw in BLOCKS_ONE:
        base = vol[192:] if sd else vol
        shift = 64 * sd + 8 * sh + sw
        if shift:
            base = pltpu.roll(base, shift, 1)
        if sh:
            base = jnp.where(p_all[: base.shape[0]] == 0, 0.0, base)
        if sw:
            base = jnp.where(q_all[: base.shape[0]] == 0, 0.0, base)
        base = base.astype(jnp.bfloat16)
        if sh:
            for md in range(base.shape[0] // 64):
                x_ref[row : row + 16] = base[md * 64 + 48 : md * 64 + 64]
                row += 16
        else:
            x_ref[row : row + base.shape[0]] = base
            row += base.shape[0]
    x_ref[row:] = jnp.zeros((SUBROWS - row, 256), jnp.bfloat16)
    p1_ref[...] = dot(sel_ref[...], x_ref[...]).astype(jnp.bfloat16)
    pre = [dot(w1_ref[...], p1_ref[ph * 128 : ph * 128 + 128]) for ph in range(8)]
    pre = jnp.concatenate(pre, axis=0)
    sig = 1.0 / (1.0 + jnp.exp(-pre))
    act = (pre * sig).astype(jnp.bfloat16).astype(jnp.float32)

    p_own, q_own = p_all[:32, :CELLS], q_all[:32, :CELLS]
    for t, tap in enumerate(TAPS):
        p2_ref[t * 32 : t * 32 + 32] = patches_two(act, p_own, q_own, tap)
    p2 = p2_ref[...]
    out_ref[...] = dot(w2_ref[...], p2).astype(jnp.bfloat16)

    cot = c_ref[...].astype(jnp.float32)
    moved = {}
    for sd, sh, sw in BLOCKS_ONE:
        shift = 64 * sd + 8 * sh + sw
        part = pltpu.roll(cot, 256 - shift, 1) if shift else cot
        part = part[:, :CELLS]
        if sh:
            part = jnp.where(p_all[:64, :CELLS] == 7, 0.0, part)
        if sw:
            part = jnp.where(q_all[:64, :CELLS] == 7, 0.0, part)
        moved[(sd, sh, sw)] = part.astype(jnp.bfloat16)
    grads = [None] * 8
    for t, (a, b, e) in enumerate(TAPS):
        ph = 4 * (a != 1) + 2 * (b != 1) + (e != 1)
        term = dot(w2t_ref[t * 32 : t * 32 + 32], moved[(int(a == 0), int(b == 0), int(e == 0))])
        grads[ph] = term if grads[ph] is None else grads[ph] + term
    grad_act = jnp.concatenate(grads, axis=0)
    pre_own, sig_own = pre[:, CELLS:], sig[:, CELLS:]
    e1 = (grad_act * (sig_own * (1.0 + pre_own * (1.0 - sig_own)))).astype(jnp.bfloat16)
    e1_ref[...] = e1

    in_one = jnp.zeros((128, 128), jnp.float32)
    grad_one = jnp.zeros((32, 128), jnp.float32)
    gram_one = jnp.zeros((32, 32), jnp.float32)
    for ph in range(8):
        p1 = p1_ref[ph * 128 : ph * 128 + 128, CELLS:]
        piece = e1[ph * 32 : ph * 32 + 32]
        in_one += dot_t(p1, p1)
        grad_one += dot_t(piece, p1)
        gram_one += dot_t(piece, piece)
    own_cot = c_ref[:, :CELLS]
    small_ref[...] = jnp.zeros((256, 128), jnp.float32)
    small_ref[0:128] = in_one
    small_ref[128:160] = grad_one
    small_ref[160:192, 0:32] = gram_one
    small_ref[192:256, 0:64] = dot_t(own_cot, own_cot)
    grad_two_ref[...] = dot_t(own_cot, p2)
    in_two_ref[...] = dot_t(p2, p2)


def halves(value):
    high = value.astype(jnp.bfloat16)
    return high, (value - high.astype(jnp.float32)).astype(jnp.bfloat16)


def times(system, direction):
    high, low = halves(direction)
    if system["left"]:
        return dot(system["high"][...], high) + (
            dot(system["high"][...], low) + dot(system["low"][...], high)
        )
    return dot(high, system["high"][...]) + (
        dot(low, system["high"][...]) + dot(high, system["low"][...])
    )


def conjugate_gradients(systems):
    def total(system, value):
        return jnp.sum(value, axis=0 if system["left"] else 1, keepdims=True)

    for system in systems:
        rhs = system["r"][...]
        system["p"][...] = rhs
        system["x"][...] = jnp.zeros_like(rhs)

    begin = [total(s, s["r"][...] * s["r"][...]) for s in systems]

    def step(carry):
        count, squares, _ = carry
        later, worst = [], jnp.float32(0.0)
        for system, square, first in zip(systems, squares, begin):
            direction = system["p"][...]
            image = times(system, direction)
            curve = total(system, direction * image)
            size = jnp.where(curve > 0.0, square / jnp.where(curve > 0.0, curve, 1.0), 0.0)
            system["x"][...] += size * direction
            rest = system["r"][...] - size * image
            system["r"][...] = rest
            fresh = total(system, rest * rest)
            turn = jnp.where(square > 0.0, fresh / jnp.where(square > 0.0, square, 1.0), 0.0)
            system["p"][...] = rest + turn * direction
            later.append(fresh)
            worst = jnp.maximum(worst, jnp.max(fresh - TOLERANCE * TOLERANCE * first))
        return count + 1, tuple(later), worst

    lax.while_loop(
        lambda carry: jnp.logical_and(carry[0] < MAX_STEPS, carry[2] > 0.0),
        step,
        (jnp.int32(0), tuple(begin), jnp.float32(1.0)),
    )


def eye(size):
    rows = lax.broadcasted_iota(jnp.int32, (size, size), 0)
    cols = lax.broadcasted_iota(jnp.int32, (size, size), 1)
    return jnp.where(rows == cols, 1.0, 0.0).astype(jnp.float32)


def solve_kernel(
    rows_one, rows_two, in_two_ref, grad_two_ref, small_ref, one_ref, two_ref,
    ah1, al1, ah2, al2, bh1, bl1, bh2, bl2, r1, p1, x1, r2, p2, x2,
):
    def put(high_ref, low_ref, value):
        high_ref[...], low_ref[...] = halves(value)

    put(ah1, al1, small_ref[0:128] * (1.0 / rows_one) + damp_input * eye(128))
    put(bh1, bl1, small_ref[160:192, 0:32] * (1.0 / rows_one) + damp_grad * eye(32))
    put(bh2, bl2, small_ref[192:256, 0:64] * (1.0 / rows_two) + damp_grad * eye(64))
    put(ah2, al2, in_two_ref[...] * (1.0 / rows_two) + damp_input * eye(in_two_ref.shape[0]))
    mean_one = small_ref[128:160] * (1.0 / rows_one)
    mean_two = grad_two_ref[...] * (1.0 / rows_two)
    r1[...] = mean_one
    r2[...] = mean_two
    conjugate_gradients([
        dict(high=ah2, low=al2, r=r2, p=p2, x=x2, left=False),
        dict(high=ah1, low=al1, r=r1, p=p1, x=x1, left=False),
    ])
    r1[...] = x1[...]
    r2[...] = x2[...]
    conjugate_gradients([
        dict(high=bh2, low=bl2, r=r2, p=p2, x=x2, left=True),
        dict(high=bh1, low=bl1, r=r1, p=p1, x=x1, left=True),
    ])
    form = jnp.sum(x1[...] * mean_one) + jnp.sum(x2[...] * mean_two)
    entries = 32 * 108 + 64 * 864
    factor = jnp.sqrt(jnp.full((1, 1), entries, jnp.float32) / form)
    one_ref[...] = factor * x1[...]
    two_ref[...] = factor * x2[...]


def passed_along(value, axis, steps):
    count = lax.axis_size(axis)
    leading, last = (max(0, -steps), min(count, count - steps))
    return lax.ppermute(value, axis, [(source, source + steps) for source in range(leading, last)])


def f32(*shape):
    return jax.ShapeDtypeStruct(shape, jnp.float32)


def bf16(*shape):
    return jax.ShapeDtypeStruct(shape, jnp.bfloat16)


def to_phases(volume):
    parts = volume.reshape(4, volume.shape[1] // 4, 4, 8, 4, 8, 4)
    return parts.transpose(2, 4, 6, 0, 1, 3, 5).reshape(256, -1)


def on_device(volume, cotangent, conv_one, conv_two):
    local = volume[0]
    cot = cotangent[0]
    halo = passed_along(local[:, 4:], "space", 1)
    cot_halo = passed_along(cot[:, :PLANE], "space", -1)
    vol = jnp.concatenate([jnp.zeros((256, PLANE), jnp.bfloat16), to_phases(halo), to_phases(local)], axis=1)
    cot_ext = jnp.concatenate([cot, cot_halo, jnp.zeros((64, PLANE), jnp.bfloat16)], axis=1)
    w1 = jnp.pad(conv_one.reshape(32, 108), ((0, 0), (0, 20)))
    taps_two = conv_two.reshape(64, 32, 27)
    w2 = taps_two.transpose(0, 2, 1).reshape(64, 864)
    w2t = taps_two.transpose(2, 1, 0).reshape(864, 64)
    sel = jnp.asarray(selection(), jnp.bfloat16)
    out_two, e1, in_two, grad_two, small = pl.pallas_call(
        local_kernel,
        out_shape=(bf16(64, CELLS), bf16(256, CELLS), f32(864, 864), f32(64, 864), f32(256, 128)),
        scratch_shapes=[
            pltpu.VMEM((SUBROWS, 256), jnp.bfloat16),
            pltpu.VMEM((1024, 256), jnp.bfloat16),
            pltpu.VMEM((864, CELLS), jnp.bfloat16),
        ],
    )(vol, cot_ext, sel, w1, w2, w2t)
    grad_pre = e1.reshape(2, 2, 2, 32, 2, 8, 8).transpose(3, 4, 0, 5, 1, 6, 2).reshape(32, 1024)

    in_two, grad_two, small = lax.psum((in_two, grad_two, small), ("dp", "space"))
    devices = lax.axis_size("dp") * lax.axis_size("space")
    one, two = pl.pallas_call(
        lambda *refs: solve_kernel(1024 * devices, CELLS * devices, *refs),
        out_shape=(f32(32, 128), f32(64, 864)),
        scratch_shapes=[
            pltpu.VMEM((n, n), jnp.bfloat16) for n in (128, 128, 864, 864, 32, 32, 64, 64)
        ]
        + [pltpu.VMEM((32, 128), jnp.float32)] * 3
        + [pltpu.VMEM((64, 864), jnp.float32)] * 3,
    )(in_two, grad_two, small)
    update_one = one[:, :108].reshape(-1)
    update_two = two.reshape(64, 27, 32).transpose(0, 2, 1).reshape(-1)
    return (out_two[None], grad_pre[None], update_one, update_two)


def solution(mesh):
    in_specs = (P("dp", None, "space", None, None), P("dp", None, "space"), P(), P())
    out_specs = (P("dp", None, "space"), P("dp", None, "space"), P(), P())
    return jax.shard_map(
        on_device, mesh=mesh, in_specs=in_specs, out_specs=out_specs, check_vma=False
    )
```

```python
import jax
import jax.numpy as jnp
import numpy as np
from jax import lax
from jax.experimental import pallas as pl
from jax.experimental.pallas import tpu as pltpu
from jax.sharding import PartitionSpec as P

damp_input = 0.1
damp_grad = 0.03
TOLERANCE = 1e-6
MAX_STEPS = 5000
CELLS = 128
PLANE = 64
BLOCKS_ONE = [(sd, sh, sw) for sd in (0, 1) for sh in (0, 1) for sw in (0, 1)]
TAPS = [(a, b, e) for a in range(3) for b in range(3) for e in range(3)]
PHASES = [(d, h, w) for d in (0, 1) for h in (0, 1) for w in (0, 1)]
SUBROWS = 896
HALF = 160
SUMS = 192
GROUP = 4


def block_rows():
    table, row = {}, 0
    for sd, sh, sw in BLOCKS_ONE:
        for md in (3,) if sd else range(4):
            for mh in (3,) if sh else range(4):
                for mw in range(4):
                    for c in range(4):
                        table[(sd, sh, sw, md, mh, mw, c)] = row
                        row += 1
    return table


def selection():
    table = block_rows()
    sel = np.zeros((8 * 128, SUBROWS), np.float32)
    for ph, (dp, hp, wp) in enumerate(PHASES):
        for c in range(4):
            for t, (a, b, e) in enumerate(TAPS):
                offs = [2 * dp + a - 1, 2 * hp + b - 1, 2 * wp + e - 1]
                sh = [int(o < 0) for o in offs]
                md = [o % 4 for o in offs]
                sel[ph * 128 + c * 27 + t, table[(*sh, *md, c)]] = 1.0
    return sel


def dot(left, right):
    return jnp.dot(left, right, preferred_element_type=jnp.float32)


def dot_t(left, right):
    return lax.dot_general(left, right, (((1,), (1,)), ((), ())), preferred_element_type=jnp.float32)


def patches_two(act, p_idx, q_idx, tap):
    a, b, e = tap
    ph = 4 * (a != 1) + 2 * (b != 1) + (e != 1)
    shift = 64 * (a == 0) + 8 * (b == 0) + (e == 0)
    rows = act[ph * 32 : ph * 32 + 32]
    if shift:
        rows = pltpu.roll(rows, shift, 1)
    rows = rows[:, CELLS:]
    if b == 0:
        rows = jnp.where(p_idx == 0, 0.0, rows)
    if e == 0:
        rows = jnp.where(q_idx == 0, 0.0, rows)
    return rows.astype(jnp.bfloat16)


def local_kernel(
    v_ref, c_ref, sel_ref, w1_ref, w2_ref, w2t_ref,
    out_ref, e1_ref, a_ref, b_ref, small_ref,
    x_ref, p1_ref, p2_ref,
):
    lane = lax.broadcasted_iota(jnp.int32, (256, 256), 1)
    p_all = (lane // 8) % 8
    q_all = lane % 8
    vol = v_ref[...].astype(jnp.float32)
    row = 0
    for sd, sh, sw in BLOCKS_ONE:
        base = vol[192:] if sd else vol
        shift = 64 * sd + 8 * sh + sw
        if shift:
            base = pltpu.roll(base, shift, 1)
        if sh:
            base = jnp.where(p_all[: base.shape[0]] == 0, 0.0, base)
        if sw:
            base = jnp.where(q_all[: base.shape[0]] == 0, 0.0, base)
        base = base.astype(jnp.bfloat16)
        if sh:
            for md in range(base.shape[0] // 64):
                x_ref[row : row + 16] = base[md * 64 + 48 : md * 64 + 64]
                row += 16
        else:
            x_ref[row : row + base.shape[0]] = base
            row += base.shape[0]
    x_ref[row:] = jnp.zeros((SUBROWS - row, 256), jnp.bfloat16)
    p1_ref[...] = dot(sel_ref[...], x_ref[...]).astype(jnp.bfloat16)
    pre = [dot(w1_ref[...], p1_ref[ph * 128 : ph * 128 + 128]) for ph in range(8)]
    pre = jnp.concatenate(pre, axis=0)
    sig = 1.0 / (1.0 + jnp.exp(-pre))
    act = (pre * sig).astype(jnp.bfloat16)
    a_ref[...] = act[:HALF, CELLS:]
    b_ref[0 : 256 - HALF] = act[HALF:, CELLS:]
    b_ref[256 - HALF :] = c_ref[:, :CELLS]
    act = act.astype(jnp.float32)

    p_own, q_own = p_all[:32, :CELLS], q_all[:32, :CELLS]
    for t, tap in enumerate(TAPS):
        p2_ref[t * 32 : t * 32 + 32] = patches_two(act, p_own, q_own, tap)
    p2 = p2_ref[...]
    out_ref[...] = dot(w2_ref[...], p2).astype(jnp.bfloat16)

    cot = c_ref[...].astype(jnp.float32)
    moved = {}
    for sd, sh, sw in BLOCKS_ONE:
        shift = 64 * sd + 8 * sh + sw
        part = pltpu.roll(cot, 256 - shift, 1) if shift else cot
        part = part[:, :CELLS]
        if sh:
            part = jnp.where(p_all[:64, :CELLS] == 7, 0.0, part)
        if sw:
            part = jnp.where(q_all[:64, :CELLS] == 7, 0.0, part)
        moved[(sd, sh, sw)] = part.astype(jnp.bfloat16)
    grads = [None] * 8
    for t, (a, b, e) in enumerate(TAPS):
        ph = 4 * (a != 1) + 2 * (b != 1) + (e != 1)
        term = dot(w2t_ref[t * 32 : t * 32 + 32], moved[(int(a == 0), int(b == 0), int(e == 0))])
        grads[ph] = term if grads[ph] is None else grads[ph] + term
    grad_act = jnp.concatenate(grads, axis=0)
    pre_own, sig_own = pre[:, CELLS:], sig[:, CELLS:]
    e1 = (grad_act * (sig_own * (1.0 + pre_own * (1.0 - sig_own)))).astype(jnp.bfloat16)
    e1_ref[...] = e1

    in_one = jnp.zeros((128, 128), jnp.float32)
    grad_one = jnp.zeros((32, 128), jnp.float32)
    gram_one = jnp.zeros((32, 32), jnp.float32)
    for ph in range(8):
        p1 = p1_ref[ph * 128 : ph * 128 + 128, CELLS:]
        piece = e1[ph * 32 : ph * 32 + 32]
        in_one += dot_t(p1, p1)
        grad_one += dot_t(piece, p1)
        gram_one += dot_t(piece, piece)
    small_ref[...] = jnp.zeros((SUMS, 128), jnp.float32)
    small_ref[0:128] = in_one
    small_ref[128:160] = grad_one
    small_ref[160:192, 0:32] = gram_one


def coordinates():
    return {"dp": lax.axis_index("dp"), "space": lax.axis_index("space")}


def bit_of(value, bit):
    return (value // 2**bit) % 2


def position(order, coords):
    return sum(bit_of(coords[axis], bit) * 2**stage for stage, (axis, bit) in enumerate(order))


def orders(count_dp, count_space):
    dp_bits = [("dp", bit) for bit in reversed(range(count_dp.bit_length() - 1))]
    space_bits = [("space", bit) for bit in reversed(range(count_space.bit_length() - 1))]
    first = dp_bits + space_bits
    second = space_bits[:-1] + dp_bits + space_bits[-1:]
    sums = space_bits[-1:] + dp_bits[::-1] + space_bits[:-1]
    return first, second, sums


def exchange_kernel(
    plan, a_ref, b_ref, small_ref, ga_ref, gb_ref, total_ref, run_ref, land_ref,
    own_sem, send_sem, recv_sem,
):
    order_a, order_b, order_s = plan
    coords = coordinates()
    stages = len(order_a)

    def partner(axis, bit):
        at = coords[axis]
        other = at + (1 - 2 * bit_of(at, bit)) * 2**bit
        return {axis: other}

    barrier = pltpu.get_barrier_semaphore()
    for axis, bit in order_a:
        pl.semaphore_signal(
            barrier, inc=1, device_id=partner(axis, bit), device_id_type=pl.DeviceIdType.MESH
        )
    spots = [position(order_a, coords), position(order_b, coords)]
    owns = []
    for k, (src, dst) in enumerate(((a_ref, ga_ref), (b_ref, gb_ref))):
        own = pltpu.make_async_copy(src, dst.at[spots[k]], own_sem.at[k])
        own.start()
        owns.append(own)
    for own in owns:
        own.wait()
    pl.semaphore_wait(barrier, stages)

    for stage in range(stages):
        copies = []
        for k, (order, ref) in enumerate(((order_a, ga_ref), (order_b, gb_ref))):
            base = (spots[k] // 2**stage) * 2**stage
            held = ref.at[pl.ds(base, 2**stage)]
            copies.append((k, order[stage], held, held))
        source = small_ref if stage == 0 else run_ref.at[stage - 1]
        copies.append((2, order_s[stage], source, land_ref.at[stage]))
        sent = []
        for k, (axis, bit), src, dst in copies:
            copy = pltpu.make_async_remote_copy(
                src_ref=src,
                dst_ref=dst,
                send_sem=send_sem.at[stage, k],
                recv_sem=recv_sem.at[stage, k],
                device_id=partner(axis, bit),
                device_id_type=pl.DeviceIdType.MESH,
            )
            copy.start()
            sent.append(copy)
        sent[2].wait()
        running = (small_ref[...] if stage == 0 else run_ref[stage - 1]) + land_ref[stage]
        if stage < stages - 1:
            run_ref[stage] = running
        else:
            total_ref[...] = running
        sent[0].wait()
        sent[1].wait()


def halves(value):
    high = value.astype(jnp.bfloat16)
    return high, (value - high.astype(jnp.float32)).astype(jnp.bfloat16)


def times(system, direction):
    high, low = halves(direction)
    if system["left"]:
        return dot(system["high"][...], high) + (
            dot(system["high"][...], low) + dot(system["low"][...], high)
        )
    return dot(high, system["high"][...]) + (
        dot(low, system["high"][...]) + dot(high, system["low"][...])
    )


def conjugate_gradients(systems):
    def total(system, value):
        return jnp.sum(value, axis=0 if system["left"] else 1, keepdims=True)

    for system in systems:
        rhs = system["r"][...]
        system["p"][...] = rhs
        system["x"][...] = jnp.zeros_like(rhs)

    begin = [total(s, s["r"][...] * s["r"][...]) for s in systems]

    def step(carry):
        count, squares, _ = carry
        later, worst = [], jnp.float32(0.0)
        for system, square, first in zip(systems, squares, begin):
            direction = system["p"][...]
            image = times(system, direction)
            curve = total(system, direction * image)
            size = jnp.where(curve > 0.0, square / jnp.where(curve > 0.0, curve, 1.0), 0.0)
            system["x"][...] += size * direction
            rest = system["r"][...] - size * image
            system["r"][...] = rest
            fresh = total(system, rest * rest)
            turn = jnp.where(square > 0.0, fresh / jnp.where(square > 0.0, square, 1.0), 0.0)
            system["p"][...] = rest + turn * direction
            later.append(fresh)
            worst = jnp.maximum(worst, jnp.max(fresh - TOLERANCE * TOLERANCE * first))
        return count + 1, tuple(later), worst

    lax.while_loop(
        lambda carry: jnp.logical_and(carry[0] < MAX_STEPS, carry[2] > 0.0),
        step,
        (jnp.int32(0), tuple(begin), jnp.float32(1.0)),
    )


def eye(size):
    rows = lax.broadcasted_iota(jnp.int32, (size, size), 0)
    cols = lax.broadcasted_iota(jnp.int32, (size, size), 1)
    return jnp.where(rows == cols, 1.0, 0.0).astype(jnp.float32)


def slab_patches(act, below, out_ref, column):
    lane = lax.broadcasted_iota(jnp.int32, (128, CELLS), 1)
    act = act.astype(jnp.float32)
    odd = act[128:]
    shifted = pltpu.roll(jnp.where(lane >= PLANE, below.astype(jnp.float32), odd), PLANE, 1)
    row0 = (lane[:32] // 8) % 8 == 0
    col0 = lane[:32] % 8 == 0
    for a, base in ((0, shifted), (1, act[:128]), (2, odd)):
        for b in range(3):
            for e in range(3):
                start = 64 * (b != 1) + 32 * (e != 1)
                rows = base[start : start + 32]
                shift = 8 * (b == 0) + (e == 0)
                if shift:
                    rows = pltpu.roll(rows, shift, 1)
                if b == 0:
                    rows = jnp.where(row0, 0.0, rows)
                if e == 0:
                    rows = jnp.where(col0, 0.0, rows)
                t = 9 * a + 3 * b + e
                out_ref[t * 32 : t * 32 + 32, column : column + CELLS] = rows.astype(jnp.bfloat16)


def solve_kernel(
    plan, counts, ga_ref, gb_ref, small_ref, one_ref, two_ref,
    ah1, al1, ah2, al2, bh1, bl1, bh2, bl2, r1, p1, x1, r2, p2, x2, cols_ref, in_two_ref, side_ref,
):
    count_dp, count_space = counts
    devices = count_dp * count_space
    rows_one, rows_two = 8 * CELLS * devices, CELLS * devices
    group = min(GROUP, count_space)

    def slab(dp, space):
        coords = {"dp": dp, "space": space}
        return ga_ref[position(plan[0], coords)], gb_ref[position(plan[1], coords)]

    def gather_group(index):
        dp, first = index % count_dp, (index // count_dp) * group
        for k in range(group):
            low, high = slab(dp, first + k)
            if k > 0:
                below = before
            else:
                a, b = slab(dp, jnp.maximum(first - 1, 0))
                below = jnp.concatenate([a[128:], b[: 256 - HALF]], axis=0)
                below = jnp.where(first > 0, below, jnp.zeros_like(below))
            act = jnp.concatenate([low, high[: 256 - HALF]], axis=0)
            before = act[128:]
            slab_patches(act, below, cols_ref, k * CELLS)
            cols_ref[864:, k * CELLS : (k + 1) * CELLS] = high[256 - HALF :]

    in_two_ref[...] = jnp.zeros_like(in_two_ref)
    side_ref[...] = jnp.zeros_like(side_ref)

    def accumulate(index, carry):
        gather_group(index)
        in_two_ref[...] += dot_t(cols_ref[:864], cols_ref[:864])
        side_ref[...] += dot_t(cols_ref[864:], cols_ref[...])
        return carry

    lax.fori_loop(0, devices // group, accumulate, 0)

    def put(high_ref, low_ref, value):
        high_ref[...], low_ref[...] = halves(value)

    put(ah1, al1, small_ref[0:128] * (1.0 / rows_one) + damp_input * eye(128))
    put(bh1, bl1, small_ref[160:192, 0:32] * (1.0 / rows_one) + damp_grad * eye(32))
    put(bh2, bl2, side_ref[:, 864:] * (1.0 / rows_two) + damp_grad * eye(64))
    put(ah2, al2, in_two_ref[...] * (1.0 / rows_two) + damp_input * eye(in_two_ref.shape[0]))
    mean_one = small_ref[128:160] * (1.0 / rows_one)
    mean_two = side_ref[:, :864] * (1.0 / rows_two)
    r1[...] = mean_one
    r2[...] = mean_two
    conjugate_gradients([
        dict(high=ah2, low=al2, r=r2, p=p2, x=x2, left=False),
        dict(high=ah1, low=al1, r=r1, p=p1, x=x1, left=False),
    ])
    r1[...] = x1[...]
    r2[...] = x2[...]
    conjugate_gradients([
        dict(high=bh2, low=bl2, r=r2, p=p2, x=x2, left=True),
        dict(high=bh1, low=bl1, r=r1, p=p1, x=x1, left=True),
    ])
    form = jnp.sum(x1[...] * mean_one) + jnp.sum(x2[...] * mean_two)
    entries = 32 * 108 + 64 * 864
    factor = jnp.sqrt(jnp.full((1, 1), entries, jnp.float32) / form)
    one_ref[...] = factor * x1[...]
    two_ref[...] = factor * x2[...]


def passed_along(value, axis, steps):
    count = lax.axis_size(axis)
    leading, last = (max(0, -steps), min(count, count - steps))
    return lax.ppermute(value, axis, [(source, source + steps) for source in range(leading, last)])


def f32(*shape):
    return jax.ShapeDtypeStruct(shape, jnp.float32)


def bf16(*shape):
    return jax.ShapeDtypeStruct(shape, jnp.bfloat16)


def to_phases(volume):
    parts = volume.reshape(4, volume.shape[1] // 4, 4, 8, 4, 8, 4)
    return parts.transpose(2, 4, 6, 0, 1, 3, 5).reshape(256, -1)


def on_device(volume, cotangent, conv_one, conv_two):
    local = volume[0]
    cot = cotangent[0]
    phases = to_phases(local)
    halo = passed_along(phases[:, PLANE:], "space", 1)
    cot_halo = passed_along(cot[:, :PLANE], "space", -1)
    vol = jnp.concatenate([jnp.zeros((256, PLANE), jnp.bfloat16), halo, phases], axis=1)
    cot_ext = jnp.concatenate([cot, cot_halo, jnp.zeros((64, PLANE), jnp.bfloat16)], axis=1)
    w1 = jnp.pad(conv_one.reshape(32, 108), ((0, 0), (0, 20)))
    taps_two = conv_two.reshape(64, 32, 27)
    w2 = taps_two.transpose(0, 2, 1).reshape(64, 864)
    w2t = taps_two.transpose(2, 1, 0).reshape(864, 64)
    sel = jnp.asarray(selection(), jnp.bfloat16)
    out_two, e1, block_a, block_b, small = pl.pallas_call(
        local_kernel,
        out_shape=(bf16(64, CELLS), bf16(256, CELLS), bf16(HALF, CELLS), bf16(320 - HALF, CELLS), f32(SUMS, 128)),
        scratch_shapes=[
            pltpu.VMEM((SUBROWS, 256), jnp.bfloat16),
            pltpu.VMEM((1024, 256), jnp.bfloat16),
            pltpu.VMEM((864, CELLS), jnp.bfloat16),
        ],
    )(vol, cot_ext, sel, w1, w2, w2t)
    grad_pre = e1.reshape(2, 2, 2, 32, 2, 8, 8).transpose(3, 4, 0, 5, 1, 6, 2).reshape(32, 1024)

    counts = (lax.axis_size("dp"), lax.axis_size("space"))
    plan = orders(*counts)
    stages = len(plan[0])
    devices = counts[0] * counts[1]
    all_a, all_b, small = pl.pallas_call(
        lambda *refs: exchange_kernel(plan, *refs),
        out_shape=(bf16(devices, HALF, CELLS), bf16(devices, 320 - HALF, CELLS), f32(SUMS, 128)),
        in_specs=[pl.BlockSpec(memory_space=pltpu.VMEM)] * 3,
        out_specs=[pl.BlockSpec(memory_space=pltpu.VMEM)] * 3,
        scratch_shapes=[
            pltpu.VMEM((stages, SUMS, 128), jnp.float32),
            pltpu.VMEM((stages, SUMS, 128), jnp.float32),
            pltpu.SemaphoreType.DMA((2,)),
            pltpu.SemaphoreType.DMA((stages, 3)),
            pltpu.SemaphoreType.DMA((stages, 3)),
        ],
        compiler_params=pltpu.CompilerParams(collective_id=0, has_side_effects=True),
    )(block_a, block_b, small)
    one, two = pl.pallas_call(
        lambda *refs: solve_kernel(plan, counts, *refs),
        out_shape=(f32(32, 128), f32(64, 864)),
        scratch_shapes=[
            pltpu.VMEM((n, n), jnp.bfloat16) for n in (128, 128, 864, 864, 32, 32, 64, 64)
        ]
        + [pltpu.VMEM((32, 128), jnp.float32)] * 3
        + [pltpu.VMEM((64, 864), jnp.float32)] * 3
        + [
            pltpu.VMEM((928, min(GROUP, counts[1]) * CELLS), jnp.bfloat16),
            pltpu.VMEM((864, 864), jnp.float32),
            pltpu.VMEM((64, 928), jnp.float32),
        ],
    )(all_a, all_b, small)
    update_one = one[:, :108].reshape(-1)
    update_two = two.reshape(64, 27, 32).transpose(0, 2, 1).reshape(-1)
    return (out_two[None], grad_pre[None], update_one, update_two)


def solution(mesh):
    in_specs = (P("dp", None, "space", None, None), P("dp", None, "space"), P(), P())
    out_specs = (P("dp", None, "space"), P("dp", None, "space"), P(), P())
    return jax.shard_map(
        on_device, mesh=mesh, in_specs=in_specs, out_specs=out_specs, check_vma=False
    )
```

```python
import jax
import jax.numpy as jnp
import numpy as np
from jax import lax
from jax.experimental import pallas as pl
from jax.experimental.pallas import tpu as pltpu
from jax.sharding import PartitionSpec as P

damp_input = 0.1
damp_grad = 0.03
TOLERANCE = 1e-6
MAX_STEPS = 5000
CELLS = 128
PLANE = 64
SHIFTS = [(sd, sh, sw) for sd in (0, 1) for sh in (0, 1) for sw in (0, 1)]
TAPS = [(a, b, e) for a in range(3) for b in range(3) for e in range(3)]
PHASES = [(d, h, w) for d in (0, 1) for h in (0, 1) for w in (0, 1)]
SUBROWS = 896
HALF = 160
SUMS = 192
GROUP = 4


def block_rows():
    table, row = {}, 0
    for sd, sh, sw in SHIFTS:
        for mw in (3,) if sw else range(4):
            for md in (3,) if sd else range(4):
                for mh in range(4):
                    for c in range(4):
                        table[(sd, sh, sw, md, mh, mw, c)] = row
                        row += 1
    return table


def column_spread():
    spread = np.zeros((32, 4, 16, 8), np.float32)
    for w in range(32):
        spread[w, w % 4, :, w // 4] = 1.0
    return spread.reshape(32, 512)


def row_sums(planes):
    sums = np.zeros((4, 4, 4, 4, planes, 32), np.float32)
    for c in range(4):
        for d in range(planes):
            for h in range(32):
                sums[d % 4, h % 4, c, c, d, h] = 1.0
    return sums.reshape(64, -1)


def selection():
    table = block_rows()
    sel = np.zeros((8 * 128, SUBROWS), np.float32)
    for ph, (dp, hp, wp) in enumerate(PHASES):
        for c in range(4):
            for t, (a, b, e) in enumerate(TAPS):
                offs = [2 * dp + a - 1, 2 * hp + b - 1, 2 * wp + e - 1]
                sh = [int(o < 0) for o in offs]
                md = [o % 4 for o in offs]
                sel[ph * 128 + c * 27 + t, table[(*sh, *md, c)]] = 1.0
    return sel


def dot(left, right):
    return jnp.dot(left, right, preferred_element_type=jnp.float32)


def dot_t(left, right):
    return lax.dot_general(left, right, (((1,), (1,)), ((), ())), preferred_element_type=jnp.float32)


def patches_two(act, p_idx, q_idx, tap):
    a, b, e = tap
    ph = 4 * (a != 1) + 2 * (b != 1) + (e != 1)
    shift = 64 * (a == 0) + 8 * (b == 0) + (e == 0)
    rows = act[ph * 32 : ph * 32 + 32]
    if shift:
        rows = pltpu.roll(rows, shift, 1)
    rows = rows[:, CELLS:]
    if b == 0:
        rows = jnp.where(p_idx == 0, 0.0, rows)
    if e == 0:
        rows = jnp.where(q_idx == 0, 0.0, rows)
    return rows.astype(jnp.bfloat16)


def volume_phases(rows, spread, sums, planes, first):
    wide = dot(rows, spread)
    row = lax.broadcasted_iota(jnp.int32, wide.shape, 0)
    lane = lax.broadcasted_iota(jnp.int32, wide.shape, 1)
    cell = first + (row % (32 * planes)) // 128
    keep = (lane % 128) // 8 == 8 * cell + (row % 32) // 4
    phases = dot(sums, jnp.where(keep, wide, 0.0).astype(jnp.bfloat16))
    return jnp.concatenate([phases[:, mw * 128 : mw * 128 + 128] for mw in range(4)], axis=0)


def local_kernel(
    v_ref, halo_ref, spread_ref, sums_ref, halo_sums_ref, c_ref, sel_ref, w1_ref, w2_ref, w2t_ref,
    out_ref, e1_ref, a_ref, b_ref, small_ref,
    x_ref, p1_ref, p2_ref,
):
    lane = lax.broadcasted_iota(jnp.int32, (256, 256), 1)
    p_all = (lane // 8) % 8
    q_all = lane % 8
    vol = jnp.concatenate(
        [
            volume_phases(halo_ref[...], spread_ref[...], halo_sums_ref[...], 4, 1),
            volume_phases(v_ref[...], spread_ref[...], sums_ref[...], 8, 0),
        ],
        axis=1,
    )
    row = 0
    for sd, sh, sw in SHIFTS:
        base = vol[192:] if sw else vol
        shift = 64 * sd + 8 * sh + sw
        if shift:
            base = pltpu.roll(base, shift, 1)
        if sh:
            base = jnp.where(p_all[: base.shape[0]] == 0, 0.0, base)
        if sw:
            base = jnp.where(q_all[: base.shape[0]] == 0, 0.0, base)
        base = base.astype(jnp.bfloat16)
        if sd:
            for mw in range(base.shape[0] // 64):
                x_ref[row : row + 16] = base[mw * 64 + 48 : mw * 64 + 64]
                row += 16
        else:
            x_ref[row : row + base.shape[0]] = base
            row += base.shape[0]
    x_ref[row:] = jnp.zeros((SUBROWS - row, 256), jnp.bfloat16)
    p1_ref[...] = dot(sel_ref[...], x_ref[...]).astype(jnp.bfloat16)
    pre = [dot(w1_ref[...], p1_ref[ph * 128 : ph * 128 + 128]) for ph in range(8)]
    pre = jnp.concatenate(pre, axis=0)
    sig = 1.0 / (1.0 + jnp.exp(-pre))
    act = (pre * sig).astype(jnp.bfloat16)
    a_ref[...] = act[:HALF, CELLS:]
    b_ref[0 : 256 - HALF] = act[HALF:, CELLS:]
    b_ref[256 - HALF :] = c_ref[:, :CELLS]
    act = act.astype(jnp.float32)

    p_own, q_own = p_all[:32, :CELLS], q_all[:32, :CELLS]
    for t, tap in enumerate(TAPS):
        p2_ref[t * 32 : t * 32 + 32] = patches_two(act, p_own, q_own, tap)
    p2 = p2_ref[...]
    out_ref[...] = dot(w2_ref[...], p2).astype(jnp.bfloat16)

    cot = c_ref[...].astype(jnp.float32)
    moved = {}
    for sd, sh, sw in SHIFTS:
        shift = 64 * sd + 8 * sh + sw
        part = pltpu.roll(cot, 256 - shift, 1) if shift else cot
        part = part[:, :CELLS]
        if sh:
            part = jnp.where(p_all[:64, :CELLS] == 7, 0.0, part)
        if sw:
            part = jnp.where(q_all[:64, :CELLS] == 7, 0.0, part)
        moved[(sd, sh, sw)] = part.astype(jnp.bfloat16)
    grads = [None] * 8
    for t, (a, b, e) in enumerate(TAPS):
        ph = 4 * (a != 1) + 2 * (b != 1) + (e != 1)
        term = dot(w2t_ref[t * 32 : t * 32 + 32], moved[(int(a == 0), int(b == 0), int(e == 0))])
        grads[ph] = term if grads[ph] is None else grads[ph] + term
    grad_act = jnp.concatenate(grads, axis=0)
    pre_own, sig_own = pre[:, CELLS:], sig[:, CELLS:]
    e1 = (grad_act * (sig_own * (1.0 + pre_own * (1.0 - sig_own)))).astype(jnp.bfloat16)
    e1_ref[...] = e1

    in_one = jnp.zeros((128, 128), jnp.float32)
    grad_one = jnp.zeros((32, 128), jnp.float32)
    gram_one = jnp.zeros((32, 32), jnp.float32)
    for ph in range(8):
        p1 = p1_ref[ph * 128 : ph * 128 + 128, CELLS:]
        piece = e1[ph * 32 : ph * 32 + 32]
        in_one += dot_t(p1, p1)
        grad_one += dot_t(piece, p1)
        gram_one += dot_t(piece, piece)
    small_ref[...] = jnp.zeros((SUMS, 128), jnp.float32)
    small_ref[0:128] = in_one
    small_ref[128:160] = grad_one
    small_ref[160:192, 0:32] = gram_one


def coordinates():
    return {"dp": lax.axis_index("dp"), "space": lax.axis_index("space")}


def bit_of(value, bit):
    return (value // 2**bit) % 2


def position(order, coords):
    return sum(bit_of(coords[axis], bit) * 2**stage for stage, (axis, bit) in enumerate(order))


def orders(count_dp, count_space):
    dp_bits = [("dp", bit) for bit in reversed(range(count_dp.bit_length() - 1))]
    space_bits = [("space", bit) for bit in reversed(range(count_space.bit_length() - 1))]
    first = dp_bits + space_bits
    second = space_bits[:-1] + dp_bits + space_bits[-1:]
    sums = space_bits[-1:] + dp_bits[::-1] + space_bits[:-1]
    return first, second, sums


def exchange_kernel(
    plan, a_ref, b_ref, small_ref, ga_ref, gb_ref, total_ref, run_ref, land_ref,
    own_sem, send_sem, recv_sem,
):
    order_a, order_b, order_s = plan
    coords = coordinates()
    stages = len(order_a)

    def partner(axis, bit):
        at = coords[axis]
        other = at + (1 - 2 * bit_of(at, bit)) * 2**bit
        return {axis: other}

    barrier = pltpu.get_barrier_semaphore()
    for axis, bit in order_a:
        pl.semaphore_signal(
            barrier, inc=1, device_id=partner(axis, bit), device_id_type=pl.DeviceIdType.MESH
        )
    spots = [position(order_a, coords), position(order_b, coords)]
    owns = []
    for k, (src, dst) in enumerate(((a_ref, ga_ref), (b_ref, gb_ref))):
        own = pltpu.make_async_copy(src, dst.at[spots[k]], own_sem.at[k])
        own.start()
        owns.append(own)
    for own in owns:
        own.wait()
    pl.semaphore_wait(barrier, stages)

    for stage in range(stages):
        copies = []
        for k, (order, ref) in enumerate(((order_a, ga_ref), (order_b, gb_ref))):
            base = (spots[k] // 2**stage) * 2**stage
            held = ref.at[pl.ds(base, 2**stage)]
            copies.append((k, order[stage], held, held))
        source = small_ref if stage == 0 else run_ref.at[stage - 1]
        copies.append((2, order_s[stage], source, land_ref.at[stage]))
        sent = []
        for k, (axis, bit), src, dst in copies:
            copy = pltpu.make_async_remote_copy(
                src_ref=src,
                dst_ref=dst,
                send_sem=send_sem.at[stage, k],
                recv_sem=recv_sem.at[stage, k],
                device_id=partner(axis, bit),
                device_id_type=pl.DeviceIdType.MESH,
            )
            copy.start()
            sent.append(copy)
        sent[2].wait()
        running = (small_ref[...] if stage == 0 else run_ref[stage - 1]) + land_ref[stage]
        if stage < stages - 1:
            run_ref[stage] = running
        else:
            total_ref[...] = running
        sent[0].wait()
        sent[1].wait()


def halves(value):
    high = value.astype(jnp.bfloat16)
    return high, (value - high.astype(jnp.float32)).astype(jnp.bfloat16)


def times(system, direction):
    high, low = halves(direction)
    if system["left"]:
        return dot(system["high"][...], high) + (
            dot(system["high"][...], low) + dot(system["low"][...], high)
        )
    rows = high.shape[0]
    both = dot(jnp.concatenate([high, low], axis=0), system["high"][...])
    return both[:rows] + (both[rows:] + dot(high, system["low"][...]))


def conjugate_gradients(systems):
    def total(system, value):
        return jnp.sum(value, axis=0 if system["left"] else 1, keepdims=True)

    for system in systems:
        rhs = system["r"][...]
        system["p"][...] = rhs
        system["x"][...] = jnp.zeros_like(rhs)

    begin = [total(s, s["r"][...] * s["r"][...]) for s in systems]

    def step(carry):
        count, squares, _ = carry
        later, worst = [], jnp.float32(0.0)
        for system, square, first in zip(systems, squares, begin):
            direction = system["p"][...]
            image = times(system, direction)
            curve = total(system, direction * image)
            size = jnp.where(curve > 0.0, square / jnp.where(curve > 0.0, curve, 1.0), 0.0)
            system["x"][...] += size * direction
            rest = system["r"][...] - size * image
            system["r"][...] = rest
            fresh = total(system, rest * rest)
            turn = jnp.where(square > 0.0, fresh / jnp.where(square > 0.0, square, 1.0), 0.0)
            system["p"][...] = rest + turn * direction
            later.append(fresh)
            worst = jnp.maximum(worst, jnp.max(fresh - TOLERANCE * TOLERANCE * first))
        return count + 1, tuple(later), worst

    lax.while_loop(
        lambda carry: jnp.logical_and(carry[0] < MAX_STEPS, carry[2] > 0.0),
        step,
        (jnp.int32(0), tuple(begin), jnp.float32(1.0)),
    )


def eye(size):
    rows = lax.broadcasted_iota(jnp.int32, (size, size), 0)
    cols = lax.broadcasted_iota(jnp.int32, (size, size), 1)
    return jnp.where(rows == cols, 1.0, 0.0).astype(jnp.float32)


def slab_patches(act, below, out_ref, column):
    lane = lax.broadcasted_iota(jnp.int32, (128, CELLS), 1)
    act = act.astype(jnp.float32)
    odd = act[128:]
    shifted = pltpu.roll(jnp.where(lane >= PLANE, below.astype(jnp.float32), odd), PLANE, 1)
    row0 = (lane[:32] // 8) % 8 == 0
    col0 = lane[:32] % 8 == 0
    for a, base in ((0, shifted), (1, act[:128]), (2, odd)):
        for b in range(3):
            for e in range(3):
                start = 64 * (b != 1) + 32 * (e != 1)
                rows = base[start : start + 32]
                shift = 8 * (b == 0) + (e == 0)
                if shift:
                    rows = pltpu.roll(rows, shift, 1)
                if b == 0:
                    rows = jnp.where(row0, 0.0, rows)
                if e == 0:
                    rows = jnp.where(col0, 0.0, rows)
                t = 9 * a + 3 * b + e
                out_ref[t * 32 : t * 32 + 32, column : column + CELLS] = rows.astype(jnp.bfloat16)


def solve_kernel(
    plan, counts, ga_ref, gb_ref, small_ref, one_ref, two_ref,
    ah1, al1, ah2, al2, bh1, bl1, bh2, bl2, r1, p1, x1, r2, p2, x2, cols_ref, in_two_ref, side_ref,
):
    count_dp, count_space = counts
    devices = count_dp * count_space
    rows_one, rows_two = 8 * CELLS * devices, CELLS * devices
    group = min(GROUP, count_space)

    def slab(dp, space):
        coords = {"dp": dp, "space": space}
        return ga_ref[position(plan[0], coords)], gb_ref[position(plan[1], coords)]

    def gather_group(index):
        dp, first = index % count_dp, (index // count_dp) * group
        for k in range(group):
            low, high = slab(dp, first + k)
            if k > 0:
                below = before
            else:
                a, b = slab(dp, jnp.maximum(first - 1, 0))
                below = jnp.concatenate([a[128:], b[: 256 - HALF]], axis=0)
                below = jnp.where(first > 0, below, jnp.zeros_like(below))
            act = jnp.concatenate([low, high[: 256 - HALF]], axis=0)
            before = act[128:]
            slab_patches(act, below, cols_ref, k * CELLS)
            cols_ref[864:, k * CELLS : (k + 1) * CELLS] = high[256 - HALF :]

    in_two_ref[...] = jnp.zeros_like(in_two_ref)
    side_ref[...] = jnp.zeros_like(side_ref)

    def accumulate(index, carry):
        gather_group(index)
        in_two_ref[...] += dot_t(cols_ref[:864], cols_ref[:864])
        side_ref[...] += dot_t(cols_ref[864:], cols_ref[...])
        return carry

    lax.fori_loop(0, devices // group, accumulate, 0)

    def put(high_ref, low_ref, value):
        high_ref[...], low_ref[...] = halves(value)

    put(ah1, al1, small_ref[0:128] * (1.0 / rows_one) + damp_input * eye(128))
    put(bh1, bl1, small_ref[160:192, 0:32] * (1.0 / rows_one) + damp_grad * eye(32))
    put(bh2, bl2, side_ref[:, 864:] * (1.0 / rows_two) + damp_grad * eye(64))
    put(ah2, al2, in_two_ref[...] * (1.0 / rows_two) + damp_input * eye(in_two_ref.shape[0]))
    mean_one = small_ref[128:160] * (1.0 / rows_one)
    mean_two = side_ref[:, :864] * (1.0 / rows_two)
    r1[...] = mean_one
    r2[...] = mean_two
    conjugate_gradients([
        dict(high=ah2, low=al2, r=r2, p=p2, x=x2, left=False),
        dict(high=ah1, low=al1, r=r1, p=p1, x=x1, left=False),
    ])
    r1[...] = x1[...]
    r2[...] = x2[...]
    conjugate_gradients([
        dict(high=bh2, low=bl2, r=r2, p=p2, x=x2, left=True),
        dict(high=bh1, low=bl1, r=r1, p=p1, x=x1, left=True),
    ])
    form = jnp.sum(x1[...] * mean_one) + jnp.sum(x2[...] * mean_two)
    entries = 32 * 108 + 64 * 864
    factor = jnp.sqrt(jnp.full((1, 1), entries, jnp.float32) / form)
    one_ref[...] = factor * x1[...]
    two_ref[...] = factor * x2[...]


def passed_along(value, axis, steps):
    count = lax.axis_size(axis)
    leading, last = (max(0, -steps), min(count, count - steps))
    return lax.ppermute(value, axis, [(source, source + steps) for source in range(leading, last)])


def f32(*shape):
    return jax.ShapeDtypeStruct(shape, jnp.float32)


def bf16(*shape):
    return jax.ShapeDtypeStruct(shape, jnp.bfloat16)


def on_device(volume, cotangent, conv_one, conv_two):
    local = volume[0]
    cot = cotangent[0]
    halo = passed_along(local[:, 4:], "space", 1).reshape(-1, 32)
    cot_halo = passed_along(cot[:, :PLANE], "space", -1)
    cot_ext = jnp.concatenate([cot, cot_halo, jnp.zeros((64, PLANE), jnp.bfloat16)], axis=1)
    w1 = jnp.pad(conv_one.reshape(32, 108), ((0, 0), (0, 20)))
    taps_two = conv_two.reshape(64, 32, 27)
    w2 = taps_two.transpose(0, 2, 1).reshape(64, 864)
    w2t = taps_two.transpose(2, 1, 0).reshape(864, 64)
    sel = jnp.asarray(selection(), jnp.bfloat16)
    spread = jnp.asarray(column_spread(), jnp.bfloat16)
    row_sums_own = jnp.asarray(row_sums(8), jnp.bfloat16)
    row_sums_halo = jnp.asarray(row_sums(4), jnp.bfloat16)
    out_two, e1, block_a, block_b, small = pl.pallas_call(
        local_kernel,
        out_shape=(bf16(64, CELLS), bf16(256, CELLS), bf16(HALF, CELLS), bf16(320 - HALF, CELLS), f32(SUMS, 128)),
        scratch_shapes=[
            pltpu.VMEM((SUBROWS, 256), jnp.bfloat16),
            pltpu.VMEM((1024, 256), jnp.bfloat16),
            pltpu.VMEM((864, CELLS), jnp.bfloat16),
        ],
    )(local.reshape(-1, 32), halo, spread, row_sums_own, row_sums_halo, cot_ext, sel, w1, w2, w2t)
    grad_pre = e1.reshape(2, 2, 2, 32, 2, 8, 8).transpose(3, 4, 0, 5, 1, 6, 2).reshape(32, 1024)

    counts = (lax.axis_size("dp"), lax.axis_size("space"))
    plan = orders(*counts)
    stages = len(plan[0])
    devices = counts[0] * counts[1]
    all_a, all_b, small = pl.pallas_call(
        lambda *refs: exchange_kernel(plan, *refs),
        out_shape=(bf16(devices, HALF, CELLS), bf16(devices, 320 - HALF, CELLS), f32(SUMS, 128)),
        in_specs=[pl.BlockSpec(memory_space=pltpu.VMEM)] * 3,
        out_specs=[pl.BlockSpec(memory_space=pltpu.VMEM)] * 3,
        scratch_shapes=[
            pltpu.VMEM((stages, SUMS, 128), jnp.float32),
            pltpu.VMEM((stages, SUMS, 128), jnp.float32),
            pltpu.SemaphoreType.DMA((2,)),
            pltpu.SemaphoreType.DMA((stages, 3)),
            pltpu.SemaphoreType.DMA((stages, 3)),
        ],
        compiler_params=pltpu.CompilerParams(collective_id=0, has_side_effects=True),
    )(block_a, block_b, small)
    one, two = pl.pallas_call(
        lambda *refs: solve_kernel(plan, counts, *refs),
        out_shape=(f32(32, 128), f32(64, 864)),
        scratch_shapes=[
            pltpu.VMEM((n, n), jnp.bfloat16) for n in (128, 128, 864, 864, 32, 32, 64, 64)
        ]
        + [pltpu.VMEM((32, 128), jnp.float32)] * 3
        + [pltpu.VMEM((64, 864), jnp.float32)] * 3
        + [
            pltpu.VMEM((928, min(GROUP, counts[1]) * CELLS), jnp.bfloat16),
            pltpu.VMEM((864, 864), jnp.float32),
            pltpu.VMEM((64, 928), jnp.float32),
        ],
    )(all_a, all_b, small)
    update_one = one[:, :108].reshape(-1)
    update_two = two.reshape(64, 27, 32).transpose(0, 2, 1).reshape(-1)
    return (out_two[None], grad_pre[None], update_one, update_two)


def solution(mesh):
    in_specs = (P("dp", None, "space", None, None), P("dp", None, "space"), P(), P())
    out_specs = (P("dp", None, "space"), P("dp", None, "space"), P(), P())
    return jax.shard_map(
        on_device, mesh=mesh, in_specs=in_specs, out_specs=out_specs, check_vma=False
    )
```

```python
import jax
import jax.numpy as jnp
import numpy as np
from jax import lax
from jax.experimental import pallas as pl
from jax.experimental.pallas import tpu as pltpu
from jax.sharding import PartitionSpec as P

damp_input = 0.1
damp_grad = 0.03
TOLERANCE = 1e-5
MAX_STEPS = 5000
CELLS = 128
PLANE = 64
SHIFTS = [(sd, sh, sw) for sd in (0, 1) for sh in (0, 1) for sw in (0, 1)]
TAPS = [(a, b, e) for a in range(3) for b in range(3) for e in range(3)]
PHASES = [(d, h, w) for d in (0, 1) for h in (0, 1) for w in (0, 1)]
SUBROWS = 896
HALF = 160
SUMS = 192
GROUP = 4


def block_rows():
    table, row = {}, 0
    for sd, sh, sw in SHIFTS:
        for mw in (3,) if sw else range(4):
            for md in (3,) if sd else range(4):
                for mh in range(4):
                    for c in range(4):
                        table[(sd, sh, sw, md, mh, mw, c)] = row
                        row += 1
    return table


def column_spread():
    spread = np.zeros((32, 4, 16, 8), np.float32)
    for w in range(32):
        spread[w, w % 4, :, w // 4] = 1.0
    return spread.reshape(32, 512)


def row_sums(planes):
    sums = np.zeros((4, 4, 4, 4, planes, 32), np.float32)
    for c in range(4):
        for d in range(planes):
            for h in range(32):
                sums[d % 4, h % 4, c, c, d, h] = 1.0
    return sums.reshape(64, -1)


def selection():
    table = block_rows()
    sel = np.zeros((8 * 128, SUBROWS), np.float32)
    for ph, (dp, hp, wp) in enumerate(PHASES):
        for c in range(4):
            for t, (a, b, e) in enumerate(TAPS):
                offs = [2 * dp + a - 1, 2 * hp + b - 1, 2 * wp + e - 1]
                sh = [int(o < 0) for o in offs]
                md = [o % 4 for o in offs]
                sel[ph * 128 + c * 27 + t, table[(*sh, *md, c)]] = 1.0
    return sel


def dot(left, right):
    return jnp.dot(left, right, preferred_element_type=jnp.float32)


def dot_t(left, right):
    return lax.dot_general(left, right, (((1,), (1,)), ((), ())), preferred_element_type=jnp.float32)


def patches_two(act, p_idx, q_idx, tap):
    a, b, e = tap
    ph = 4 * (a != 1) + 2 * (b != 1) + (e != 1)
    shift = 64 * (a == 0) + 8 * (b == 0) + (e == 0)
    rows = act[ph * 32 : ph * 32 + 32]
    if shift:
        rows = pltpu.roll(rows, shift, 1)
    rows = rows[:, CELLS:]
    if b == 0:
        rows = jnp.where(p_idx == 0, 0.0, rows)
    if e == 0:
        rows = jnp.where(q_idx == 0, 0.0, rows)
    return rows.astype(jnp.bfloat16)


def volume_phases(rows, spread, sums, planes, first):
    wide = dot(rows, spread)
    row = lax.broadcasted_iota(jnp.int32, wide.shape, 0)
    lane = lax.broadcasted_iota(jnp.int32, wide.shape, 1)
    cell = first + (row % (32 * planes)) // 128
    keep = (lane % 128) // 8 == 8 * cell + (row % 32) // 4
    phases = dot(sums, jnp.where(keep, wide, 0.0).astype(jnp.bfloat16))
    return jnp.concatenate([phases[:, mw * 128 : mw * 128 + 128] for mw in range(4)], axis=0)


def local_kernel(
    v_ref, halo_ref, spread_ref, sums_ref, halo_sums_ref, c_ref, sel_ref, w1_ref, w2_ref, w2t_ref,
    out_ref, e1_ref, a_ref, b_ref, small_ref,
    x_ref, p1_ref, p2_ref,
):
    lane = lax.broadcasted_iota(jnp.int32, (256, 256), 1)
    p_all = (lane // 8) % 8
    q_all = lane % 8
    vol = jnp.concatenate(
        [
            volume_phases(halo_ref[...], spread_ref[...], halo_sums_ref[...], 4, 1),
            volume_phases(v_ref[...], spread_ref[...], sums_ref[...], 8, 0),
        ],
        axis=1,
    )
    row = 0
    for sd, sh, sw in SHIFTS:
        base = vol[192:] if sw else vol
        shift = 64 * sd + 8 * sh + sw
        if shift:
            base = pltpu.roll(base, shift, 1)
        if sh:
            base = jnp.where(p_all[: base.shape[0]] == 0, 0.0, base)
        if sw:
            base = jnp.where(q_all[: base.shape[0]] == 0, 0.0, base)
        base = base.astype(jnp.bfloat16)
        if sd:
            for mw in range(base.shape[0] // 64):
                x_ref[row : row + 16] = base[mw * 64 + 48 : mw * 64 + 64]
                row += 16
        else:
            x_ref[row : row + base.shape[0]] = base
            row += base.shape[0]
    x_ref[row:] = jnp.zeros((SUBROWS - row, 256), jnp.bfloat16)
    p1_ref[...] = dot(sel_ref[...], x_ref[...]).astype(jnp.bfloat16)
    pre = [dot(w1_ref[...], p1_ref[ph * 128 : ph * 128 + 128]) for ph in range(8)]
    pre = jnp.concatenate(pre, axis=0)
    sig = 1.0 / (1.0 + jnp.exp(-pre))
    act = (pre * sig).astype(jnp.bfloat16)
    a_ref[...] = act[:HALF, CELLS:]
    b_ref[0 : 256 - HALF] = act[HALF:, CELLS:]
    b_ref[256 - HALF :] = c_ref[:, :CELLS]
    act = act.astype(jnp.float32)

    p_own, q_own = p_all[:32, :CELLS], q_all[:32, :CELLS]
    for t, tap in enumerate(TAPS):
        p2_ref[t * 32 : t * 32 + 32] = patches_two(act, p_own, q_own, tap)
    p2 = p2_ref[...]
    out_ref[...] = dot(w2_ref[...], p2).astype(jnp.bfloat16)

    cot = c_ref[...].astype(jnp.float32)
    moved = {}
    for sd, sh, sw in SHIFTS:
        shift = 64 * sd + 8 * sh + sw
        part = pltpu.roll(cot, 256 - shift, 1) if shift else cot
        part = part[:, :CELLS]
        if sh:
            part = jnp.where(p_all[:64, :CELLS] == 7, 0.0, part)
        if sw:
            part = jnp.where(q_all[:64, :CELLS] == 7, 0.0, part)
        moved[(sd, sh, sw)] = part.astype(jnp.bfloat16)
    grads = [None] * 8
    for t, (a, b, e) in enumerate(TAPS):
        ph = 4 * (a != 1) + 2 * (b != 1) + (e != 1)
        term = dot(w2t_ref[t * 32 : t * 32 + 32], moved[(int(a == 0), int(b == 0), int(e == 0))])
        grads[ph] = term if grads[ph] is None else grads[ph] + term
    grad_act = jnp.concatenate(grads, axis=0)
    pre_own, sig_own = pre[:, CELLS:], sig[:, CELLS:]
    e1 = (grad_act * (sig_own * (1.0 + pre_own * (1.0 - sig_own)))).astype(jnp.bfloat16)
    e1_ref[...] = e1

    in_one = jnp.zeros((128, 128), jnp.float32)
    grad_one = jnp.zeros((32, 128), jnp.float32)
    gram_one = jnp.zeros((32, 32), jnp.float32)
    for ph in range(8):
        p1 = p1_ref[ph * 128 : ph * 128 + 128, CELLS:]
        piece = e1[ph * 32 : ph * 32 + 32]
        in_one += dot_t(p1, p1)
        grad_one += dot_t(piece, p1)
        gram_one += dot_t(piece, piece)
    small_ref[...] = jnp.zeros((SUMS, 128), jnp.float32)
    small_ref[0:128] = in_one
    small_ref[128:160] = grad_one
    small_ref[160:192, 0:32] = gram_one


def coordinates():
    return {"dp": lax.axis_index("dp"), "space": lax.axis_index("space")}


def bit_of(value, bit):
    return (value // 2**bit) % 2


def position(order, coords):
    return sum(bit_of(coords[axis], bit) * 2**stage for stage, (axis, bit) in enumerate(order))


def orders(count_dp, count_space):
    dp_bits = [("dp", bit) for bit in reversed(range(count_dp.bit_length() - 1))]
    space_bits = [("space", bit) for bit in reversed(range(count_space.bit_length() - 1))]
    first = dp_bits + space_bits
    second = space_bits[:-1] + dp_bits + space_bits[-1:]
    sums = space_bits[-1:] + dp_bits[::-1] + space_bits[:-1]
    return first, second, sums


def exchange_kernel(
    plan, a_ref, b_ref, small_ref, ga_ref, gb_ref, total_ref, run_ref, land_ref,
    own_sem, send_sem, recv_sem,
):
    order_a, order_b, order_s = plan
    coords = coordinates()
    stages = len(order_a)

    def partner(axis, bit):
        at = coords[axis]
        other = at + (1 - 2 * bit_of(at, bit)) * 2**bit
        return {axis: other}

    barrier = pltpu.get_barrier_semaphore()
    for axis, bit in order_a:
        pl.semaphore_signal(
            barrier, inc=1, device_id=partner(axis, bit), device_id_type=pl.DeviceIdType.MESH
        )
    spots = [position(order_a, coords), position(order_b, coords)]
    owns = []
    for k, (src, dst) in enumerate(((a_ref, ga_ref), (b_ref, gb_ref))):
        own = pltpu.make_async_copy(src, dst.at[spots[k]], own_sem.at[k])
        own.start()
        owns.append(own)
    for own in owns:
        own.wait()
    pl.semaphore_wait(barrier, stages)

    for stage in range(stages):
        copies = []
        for k, (order, ref) in enumerate(((order_a, ga_ref), (order_b, gb_ref))):
            base = (spots[k] // 2**stage) * 2**stage
            held = ref.at[pl.ds(base, 2**stage)]
            copies.append((k, order[stage], held, held))
        source = small_ref if stage == 0 else run_ref.at[stage - 1]
        copies.append((2, order_s[stage], source, land_ref.at[stage]))
        sent = []
        for k, (axis, bit), src, dst in copies:
            copy = pltpu.make_async_remote_copy(
                src_ref=src,
                dst_ref=dst,
                send_sem=send_sem.at[stage, k],
                recv_sem=recv_sem.at[stage, k],
                device_id=partner(axis, bit),
                device_id_type=pl.DeviceIdType.MESH,
            )
            copy.start()
            sent.append(copy)
        sent[2].wait()
        running = (small_ref[...] if stage == 0 else run_ref[stage - 1]) + land_ref[stage]
        if stage < stages - 1:
            run_ref[stage] = running
        else:
            total_ref[...] = running
        sent[0].wait()
        sent[1].wait()


def halves(value):
    high = value.astype(jnp.bfloat16)
    return high, (value - high.astype(jnp.float32)).astype(jnp.bfloat16)


def times(system, direction):
    high, low = halves(direction)
    if system["left"]:
        return dot(system["high"][...], high) + (
            dot(system["high"][...], low) + dot(system["low"][...], high)
        )
    rows = high.shape[0]
    both = dot(jnp.concatenate([high, low], axis=0), system["high"][...])
    return both[:rows] + (both[rows:] + dot(high, system["low"][...]))


def conjugate_gradients(systems):
    def total(system, value):
        return jnp.sum(value, axis=0 if system["left"] else 1, keepdims=True)

    for system in systems:
        rhs = system["r"][...]
        system["p"][...] = rhs
        system["x"][...] = jnp.zeros_like(rhs)

    begin = [total(s, s["r"][...] * s["r"][...]) for s in systems]

    def step(carry):
        count, squares, _ = carry
        later, worst = [], jnp.float32(0.0)
        for system, square, first in zip(systems, squares, begin):
            direction = system["p"][...]
            image = times(system, direction)
            curve = total(system, direction * image)
            size = jnp.where(curve > 0.0, square / jnp.where(curve > 0.0, curve, 1.0), 0.0)
            system["x"][...] += size * direction
            rest = system["r"][...] - size * image
            system["r"][...] = rest
            fresh = total(system, rest * rest)
            turn = jnp.where(square > 0.0, fresh / jnp.where(square > 0.0, square, 1.0), 0.0)
            system["p"][...] = rest + turn * direction
            later.append(fresh)
            worst = jnp.maximum(worst, jnp.max(fresh - TOLERANCE * TOLERANCE * first))
        return count + 1, tuple(later), worst

    lax.while_loop(
        lambda carry: jnp.logical_and(carry[0] < MAX_STEPS, carry[2] > 0.0),
        step,
        (jnp.int32(0), tuple(begin), jnp.float32(1.0)),
    )


def eye(size):
    rows = lax.broadcasted_iota(jnp.int32, (size, size), 0)
    cols = lax.broadcasted_iota(jnp.int32, (size, size), 1)
    return jnp.where(rows == cols, 1.0, 0.0).astype(jnp.float32)


def slab_patches(act, below, out_ref, column):
    lane = lax.broadcasted_iota(jnp.int32, (128, CELLS), 1)
    act = act.astype(jnp.float32)
    odd = act[128:]
    shifted = pltpu.roll(jnp.where(lane >= PLANE, below.astype(jnp.float32), odd), PLANE, 1)
    row0 = (lane[:32] // 8) % 8 == 0
    col0 = lane[:32] % 8 == 0
    for a, base in ((0, shifted), (1, act[:128]), (2, odd)):
        for b in range(3):
            for e in range(3):
                start = 64 * (b != 1) + 32 * (e != 1)
                rows = base[start : start + 32]
                shift = 8 * (b == 0) + (e == 0)
                if shift:
                    rows = pltpu.roll(rows, shift, 1)
                if b == 0:
                    rows = jnp.where(row0, 0.0, rows)
                if e == 0:
                    rows = jnp.where(col0, 0.0, rows)
                t = 9 * a + 3 * b + e
                out_ref[t * 32 : t * 32 + 32, column : column + CELLS] = rows.astype(jnp.bfloat16)


def solve_kernel(
    plan, counts, ga_ref, gb_ref, small_ref, one_ref, two_ref,
    ah1, al1, ah2, al2, bh1, bl1, bh2, bl2, r1, p1, x1, r2, p2, x2, cols_ref, in_two_ref, side_ref,
):
    count_dp, count_space = counts
    devices = count_dp * count_space
    rows_one, rows_two = 8 * CELLS * devices, CELLS * devices
    group = min(GROUP, count_space)

    def slab(dp, space):
        coords = {"dp": dp, "space": space}
        return ga_ref[position(plan[0], coords)], gb_ref[position(plan[1], coords)]

    def gather_group(index):
        dp, first = index % count_dp, (index // count_dp) * group
        for k in range(group):
            low, high = slab(dp, first + k)
            if k > 0:
                below = before
            else:
                a, b = slab(dp, jnp.maximum(first - 1, 0))
                below = jnp.concatenate([a[128:], b[: 256 - HALF]], axis=0)
                below = jnp.where(first > 0, below, jnp.zeros_like(below))
            act = jnp.concatenate([low, high[: 256 - HALF]], axis=0)
            before = act[128:]
            slab_patches(act, below, cols_ref, k * CELLS)
            cols_ref[864:, k * CELLS : (k + 1) * CELLS] = high[256 - HALF :]

    in_two_ref[...] = jnp.zeros_like(in_two_ref)
    side_ref[...] = jnp.zeros_like(side_ref)

    def accumulate(index, carry):
        gather_group(index)
        for start in range(0, 864, 256):
            stop = min(start + 256, 864)
            in_two_ref[start:stop, start:] += dot_t(cols_ref[start:stop], cols_ref[start:864])
        side_ref[...] += dot_t(cols_ref[864:], cols_ref[...])
        return carry

    lax.fori_loop(0, devices // group, accumulate, 0)
    for start in range(0, 864, 256):
        for other in range(start + 256, 864, 256):
            end = min(other + 256, 864)
            in_two_ref[other:end, start : start + 256] = in_two_ref[start : start + 256, other:end].T

    def put(high_ref, low_ref, value):
        high_ref[...], low_ref[...] = halves(value)

    put(ah1, al1, small_ref[0:128] * (1.0 / rows_one) + damp_input * eye(128))
    put(bh1, bl1, small_ref[160:192, 0:32] * (1.0 / rows_one) + damp_grad * eye(32))
    put(bh2, bl2, side_ref[:, 864:] * (1.0 / rows_two) + damp_grad * eye(64))
    put(ah2, al2, in_two_ref[...] * (1.0 / rows_two) + damp_input * eye(in_two_ref.shape[0]))
    mean_one = small_ref[128:160] * (1.0 / rows_one)
    mean_two = side_ref[:, :864] * (1.0 / rows_two)
    r1[...] = mean_one
    r2[...] = mean_two
    conjugate_gradients([
        dict(high=ah2, low=al2, r=r2, p=p2, x=x2, left=False),
        dict(high=ah1, low=al1, r=r1, p=p1, x=x1, left=False),
    ])
    r1[...] = x1[...]
    r2[...] = x2[...]
    conjugate_gradients([
        dict(high=bh2, low=bl2, r=r2, p=p2, x=x2, left=True),
        dict(high=bh1, low=bl1, r=r1, p=p1, x=x1, left=True),
    ])
    form = jnp.sum(x1[...] * mean_one) + jnp.sum(x2[...] * mean_two)
    entries = 32 * 108 + 64 * 864
    factor = jnp.sqrt(jnp.full((1, 1), entries, jnp.float32) / form)
    one_ref[...] = factor * x1[...]
    two_ref[...] = factor * x2[...]


def passed_along(value, axis, steps):
    count = lax.axis_size(axis)
    leading, last = (max(0, -steps), min(count, count - steps))
    return lax.ppermute(value, axis, [(source, source + steps) for source in range(leading, last)])


def f32(*shape):
    return jax.ShapeDtypeStruct(shape, jnp.float32)


def bf16(*shape):
    return jax.ShapeDtypeStruct(shape, jnp.bfloat16)


def on_device(volume, cotangent, conv_one, conv_two):
    local = volume[0]
    cot = cotangent[0]
    halo = passed_along(local[:, 4:], "space", 1).reshape(-1, 32)
    cot_halo = passed_along(cot[:, :PLANE], "space", -1)
    cot_ext = jnp.concatenate([cot, cot_halo, jnp.zeros((64, PLANE), jnp.bfloat16)], axis=1)
    w1 = jnp.pad(conv_one.reshape(32, 108), ((0, 0), (0, 20)))
    taps_two = conv_two.reshape(64, 32, 27)
    w2 = taps_two.transpose(0, 2, 1).reshape(64, 864)
    w2t = taps_two.transpose(2, 1, 0).reshape(864, 64)
    sel = jnp.asarray(selection(), jnp.bfloat16)
    spread = jnp.asarray(column_spread(), jnp.bfloat16)
    row_sums_own = jnp.asarray(row_sums(8), jnp.bfloat16)
    row_sums_halo = jnp.asarray(row_sums(4), jnp.bfloat16)
    out_two, e1, block_a, block_b, small = pl.pallas_call(
        local_kernel,
        out_shape=(bf16(64, CELLS), bf16(256, CELLS), bf16(HALF, CELLS), bf16(320 - HALF, CELLS), f32(SUMS, 128)),
        scratch_shapes=[
            pltpu.VMEM((SUBROWS, 256), jnp.bfloat16),
            pltpu.VMEM((1024, 256), jnp.bfloat16),
            pltpu.VMEM((864, CELLS), jnp.bfloat16),
        ],
    )(local.reshape(-1, 32), halo, spread, row_sums_own, row_sums_halo, cot_ext, sel, w1, w2, w2t)
    grad_pre = e1.reshape(2, 2, 2, 32, 2, 8, 8).transpose(3, 4, 0, 5, 1, 6, 2).reshape(32, 1024)

    counts = (lax.axis_size("dp"), lax.axis_size("space"))
    plan = orders(*counts)
    stages = len(plan[0])
    devices = counts[0] * counts[1]
    all_a, all_b, small = pl.pallas_call(
        lambda *refs: exchange_kernel(plan, *refs),
        out_shape=(bf16(devices, HALF, CELLS), bf16(devices, 320 - HALF, CELLS), f32(SUMS, 128)),
        in_specs=[pl.BlockSpec(memory_space=pltpu.VMEM)] * 3,
        out_specs=[pl.BlockSpec(memory_space=pltpu.VMEM)] * 3,
        scratch_shapes=[
            pltpu.VMEM((stages, SUMS, 128), jnp.float32),
            pltpu.VMEM((stages, SUMS, 128), jnp.float32),
            pltpu.SemaphoreType.DMA((2,)),
            pltpu.SemaphoreType.DMA((stages, 3)),
            pltpu.SemaphoreType.DMA((stages, 3)),
        ],
        compiler_params=pltpu.CompilerParams(collective_id=0, has_side_effects=True),
    )(block_a, block_b, small)
    one, two = pl.pallas_call(
        lambda *refs: solve_kernel(plan, counts, *refs),
        out_shape=(f32(32, 128), f32(64, 864)),
        scratch_shapes=[
            pltpu.VMEM((n, n), jnp.bfloat16) for n in (128, 128, 864, 864, 32, 32, 64, 64)
        ]
        + [pltpu.VMEM((32, 128), jnp.float32)] * 3
        + [pltpu.VMEM((64, 864), jnp.float32)] * 3
        + [
            pltpu.VMEM((928, min(GROUP, counts[1]) * CELLS), jnp.bfloat16),
            pltpu.VMEM((864, 864), jnp.float32),
            pltpu.VMEM((64, 928), jnp.float32),
        ],
    )(all_a, all_b, small)
    update_one = one[:, :108].reshape(-1)
    update_two = two.reshape(64, 27, 32).transpose(0, 2, 1).reshape(-1)
    return (out_two[None], grad_pre[None], update_one, update_two)


def solution(mesh):
    in_specs = (P("dp", None, "space", None, None), P("dp", None, "space"), P(), P())
    out_specs = (P("dp", None, "space"), P("dp", None, "space"), P(), P())
    return jax.shard_map(
        on_device, mesh=mesh, in_specs=in_specs, out_specs=out_specs, check_vma=False
    )
```
